256 devices in a mesh: gx: 16 (over x, z_hi, core), gy: 4 (over z_lo), gz: 4 (over y).
Axes of the slice: x: 4, y: 4, z: 8 (z_hi: 2, z_lo: 4; z = z_hi * 4 + z_lo), core: 2. Of those that a mesh axis runs over, the one named last changes fastest.
Arguments:
- u_start: float32 [64, 256, 512], P('gx', 'gy', 'gz'), may hold values from 0 to 1
- v_start: float32 [64, 256, 512], P('gx', 'gy', 'gz'), may hold values from 0 to 1
- w_start: float32 [64, 256, 512], P('gx', 'gy', 'gz'), may hold values from 0 to 1
- conduct: float32 [64, 256, 512], P('gx', 'gy', 'gz'), may hold values from 0.02 to 0.14
- direction: float32 [64, 256, 512], P('gx', 'gy', 'gz'), may hold values from -2.4 to 2.4
- obs_weight: float32 [64, 256, 512], P('gx', 'gy', 'gz'), may hold values from 0.25 to 12, as said below
- tissue: int32 [64, 256, 512], P('gx', 'gy', 'gz'), may hold values from 0 to 2
- stim_x: int32 [16], replicated, may hold values from 0 to 63
- stim_y: int32 [16], replicated, may hold values from 0 to 255
- stim_z: int32 [16], replicated, may hold values from 0 to 511
- stim_step: int32 [16], replicated, may hold values from 0 to 3
Outputs:
- hess_vec: float32 [64, 256, 512], P('gx', 'gy', 'gz')
- curvature: float32 [], replicated
The draws below stay inside these ranges and needn't reach their ends.
Inputs may be any that keep to these rules, and one draw needn't show every extreme that they name: 0 marks scar, 1 healthy tissue, 2 tissue with fibers along the first dimension. `obs_weight`: positive weights.
All inputs are finite; a program needn't handle non-finite values.
Results may differ from the reference program's by a relative error of at most 0.0003.
Values sent between devices are 32-bit elements; how exact they have to be, the bound alone decides.
No kernel may reach another device: no remote copies, remote signals or barrier semaphores. Data moves between devices by JAX's collectives and lax.ppermute only.
A program may use at most 64 MiB of HBM per device.

```python
import math
from functools import partial
import jax
import jax.numpy as jnp
from jax import lax

STEPS = 4
NSTIM = 16
NX = 64
NY = 256
NZ = 512


def draw_obs_weight(key, part):
    lowest = math.log(0.25)
    ramp_x = 1.0 + 2.0 * jnp.arange(NX, dtype=jnp.float32) / max(NX - 1, 1)
    base = jnp.exp(jax.random.uniform(key, (NX, NY, NZ), jnp.float32, lowest, math.log(4.0)))
    return base * ramp_x[:, None, None]


def touch_ends(entries, rng, smallest, largest):
    extent = entries.shape
    place = [jax.random.randint(jax.random.fold_in(rng, axis), (), 0, extent[axis]) for axis in range(len(extent))]
    entries = entries.at[tuple(place)].set(smallest)
    longest = extent.index(max(extent))
    place[longest] = (place[longest] + 1) % extent[longest]
    return entries.at[tuple(place)].set(largest)


def level_of(key, extent, split, low, top_value):
    def one(axis_at, blocks):
        heights = jax.random.uniform(jax.random.fold_in(jax.random.fold_in(key, 6), axis_at), (blocks,), jnp.float32, low / len(split), top_value / len(split))
        return jnp.repeat(jnp.exp(heights), extent[axis_at] // blocks).reshape((-1,) + (1,) * (len(extent) - axis_at - 1))

    level = one(*split[0])
    for cut in split[1:]:
        level = level * one(*cut)
    return level


def noise(key, extent, scale, reach, shards=(), kind=jnp.bfloat16):
    factor_of = level_of(key, extent, shards, -0.22, 0.18) if shards else 1.0
    values = jax.random.normal(key, extent, jnp.float32) * scale * factor_of
    return jnp.minimum(jnp.maximum(values, -reach), reach).astype(kind)


def setup_inputs(seed: int = 0) -> dict:
    streams_of = jax.random.split(jax.random.key(seed), 12)
    return {
        "u_start": jnp.clip(1.0 * jax.random.uniform(streams_of[0], (NX, NY, NZ), jnp.float32) ** level_of(streams_of[0], (NX, NY, NZ), ((0, 16), (1, 4), (2, 4)), -0.2, 0.2), 0.0, 1.0),
        "v_start": jnp.clip(1.0 * jax.random.uniform(streams_of[1], (NX, NY, NZ), jnp.float32) ** level_of(streams_of[1], (NX, NY, NZ), ((0, 16), (1, 4), (2, 4)), -0.2, 0.2), 0.0, 1.0),
        "w_start": jnp.clip(1.0 * jax.random.uniform(streams_of[2], (NX, NY, NZ), jnp.float32) ** level_of(streams_of[2], (NX, NY, NZ), ((0, 16), (1, 4), (2, 4)), -0.2, 0.2), 0.0, 1.0),
        "conduct": jnp.clip(jnp.exp(math.log(0.14) - 1.9459102 * jax.random.uniform(streams_of[3], (NX, NY, NZ), jnp.float32) ** level_of(streams_of[3], (NX, NY, NZ), ((0, 16), (1, 4), (2, 4)), -0.2, 0.2)), 0.02, 0.14),
        "direction": noise(streams_of[4], (NX, NY, NZ), 0.3, 2.4, ((0, 16), (1, 4), (2, 4)), jnp.float32),
        "obs_weight": draw_obs_weight(jax.random.fold_in(streams_of[11], 71), 0),
        "tissue": touch_ends(jax.random.randint(streams_of[6], (NX, NY, NZ), 0, 3), jax.random.fold_in(streams_of[6], 1), 0, 2).astype(jnp.int32),
        "stim_x": touch_ends(jax.random.randint(streams_of[7], (NSTIM,), 0, NX), jax.random.fold_in(streams_of[7], 1), 0, NX - 1).astype(jnp.int32),
        "stim_y": touch_ends(jax.random.randint(streams_of[8], (NSTIM,), 0, NY), jax.random.fold_in(streams_of[8], 1), 0, NY - 1).astype(jnp.int32),
        "stim_z": touch_ends(jax.random.randint(streams_of[9], (NSTIM,), 0, NZ), jax.random.fold_in(streams_of[9], 1), 0, NZ - 1).astype(jnp.int32),
        "stim_step": touch_ends(jax.random.randint(streams_of[10], (NSTIM,), 0, STEPS), jax.random.fold_in(streams_of[10], 1), 0, STEPS - 1).astype(jnp.int32),
    }


time_step = 0.25
u_crit = 0.13
u_gate = 0.04
switch_width = 0.05
tau_fast = 0.4
tau_open = 12.5
tau_repol = 33.33
tau_slow = 15.0
k_slow = 10.0
u_slow = 0.85
tau_vplus = 3.33
tau_vminus_one = 19.6
tau_vminus_two = 1000.0
tau_wplus = 667.0
tau_wminus = 11.0
stim_amp = 2.0
tv_weight = 0.05
tv_smooth = 0.02

def switch(value):
    return 0.5 * (1.0 + jnp.tanh(value / switch_width))

def react(u_cell, v_gate, w_gate, stim_count):
    opened = switch(u_cell - u_crit)
    partly = switch(u_cell - u_gate)
    fast_in = -v_gate * opened * (1.0 - u_cell) * (u_cell - u_crit) / tau_fast
    slow_out = u_cell * (1.0 - opened) / tau_open + opened / tau_repol
    slow_in = -w_gate * (1.0 + jnp.tanh(k_slow * (u_cell - u_slow))) / (2.0 * tau_slow)
    u_next = u_cell + time_step * (stim_amp * stim_count - (fast_in + slow_out + slow_in))
    closed = 1.0 - opened
    v_rate = opened / tau_vplus + closed / (partly * tau_vminus_one + (1.0 - partly) * tau_vminus_two)
    w_rate = opened / tau_wplus + closed / tau_wminus
    v_next = closed + (v_gate - closed) * jnp.exp(-time_step * v_rate)
    w_next = closed + (w_gate - closed) * jnp.exp(-time_step * w_rate)
    return (u_next, v_next, w_next)

def kappas(tissue):
    scar = (tissue == 0).astype(jnp.float32)
    healthy = (tissue == 1).astype(jnp.float32)
    fiber = (tissue == 2).astype(jnp.float32)
    return (0.1 * scar + healthy + 1.5 * fiber, 0.1 * scar + healthy + 0.75 * fiber)

def shifted(padded, axis, offset):
    index = [slice(1, padded.shape[0] - 1), slice(1, padded.shape[1] - 1), slice(1, padded.shape[2] - 1)]
    index[axis] = slice(1 + offset, padded.shape[axis] - 1 + offset)
    return padded[tuple(index)]

def spread(along_c, across_c, live, values):
    centre = shifted(values, 0, 0)
    result = jnp.zeros(centre.shape, jnp.float32)
    for axis in range(3):
        coeff = along_c if axis == 0 else across_c
        own = shifted(coeff, axis, 0)
        for offset in (1, -1):
            face = 0.5 * (own + shifted(coeff, axis, offset)) * shifted(live, axis, offset)
            result = result + face * (shifted(values, axis, offset) - centre)
    return result

def sigma_term(along, across, live, u_pad, adj_pad):
    u_centre = shifted(u_pad, 0, 0)
    a_centre = shifted(adj_pad, 0, 0)
    parts = []
    for axis in range(3):
        part_sum = jnp.zeros(u_centre.shape, jnp.float32)
        for offset in (1, -1):
            part_sum = part_sum + 0.5 * (shifted(u_pad, axis, offset) - u_centre) * (a_centre - shifted(adj_pad, axis, offset)) * shifted(live, axis, offset)
        parts.append(part_sum)
    return along * parts[0] + across * (parts[1] + parts[2])

def forward_diff(padded, live, axis):
    lower = [slice(0, -1), slice(0, -1), slice(0, -1)]
    upper = [slice(0, -1), slice(0, -1), slice(0, -1)]
    upper[axis] = slice(1, None)
    return (padded[tuple(upper)] - padded[tuple(lower)]) * live[tuple(upper)] * live[tuple(lower)]

def tv_apply(sig_pad, dir_pad, live):
    diffs = [forward_diff(sig_pad, live, axis) for axis in range(3)]
    weight = 1.0 / jnp.sqrt(diffs[0] * diffs[0] + diffs[1] * diffs[1] + diffs[2] * diffs[2] + tv_smooth * tv_smooth)
    result = None
    for axis in range(3):
        flux = weight * forward_diff(dir_pad, live, axis)
        here = flux[1:, 1:, 1:]
        index = [slice(1, None), slice(1, None), slice(1, None)]
        index[axis] = slice(0, -1)
        term = flux[tuple(index)] - here
        result = term if result is None else result + term
    return result

def stimulus(step, xs_coord, ys_coord, zs_coord, stim_x, stim_y, stim_z, stim_step):
    active = (stim_step == step).astype(jnp.float32)
    near_x = (jnp.abs(xs_coord[None, :] - stim_x[:, None]) <= 1).astype(jnp.float32) * active[:, None]
    near_y = (jnp.abs(ys_coord[None, :] - stim_y[:, None]) <= 1).astype(jnp.float32)
    near_z = (jnp.abs(zs_coord[None, :] - stim_z[:, None]) <= 1).astype(jnp.float32)
    return jnp.einsum('si,sj,sk->ijk', near_x, near_y, near_z, precision=lax.Precision.HIGHEST)

def pad_one(array):
    return jnp.pad(array, 1)

def reference(u_start, v_start, w_start, conduct, direction, obs_weight, tissue, stim_x, stim_y, stim_z, stim_step):
    along, across = kappas(tissue)
    live = pad_one(jnp.ones(conduct.shape, jnp.float32))
    sig_pad = pad_one(conduct)
    dir_pad = pad_one(direction)
    along_pad = pad_one(along)
    across_pad = pad_one(across)
    c_along = along_pad * sig_pad
    c_across = across_pad * sig_pad
    d_along = along_pad * dir_pad
    d_across = across_pad * dir_pad
    xs_coord = jnp.arange(NX, dtype=jnp.int32)
    ys_coord = jnp.arange(NY, dtype=jnp.int32)
    zs_coord = jnp.arange(NZ, dtype=jnp.int32)
    u_cell, v_gate, w_gate = (u_start, v_start, w_start)
    du_cell = jnp.zeros(u_start.shape, jnp.float32)
    dv_gate = jnp.zeros(u_start.shape, jnp.float32)
    dw_gate = jnp.zeros(u_start.shape, jnp.float32)
    u_saved, v_saved, w_saved, du_saved = ([], [], [], [])
    for step in range(STEPS):
        u_pad = pad_one(u_cell)
        du_pad = pad_one(du_cell)
        u_saved.append(u_pad)
        v_saved.append(v_gate)
        w_saved.append(w_gate)
        stim_now = stimulus(step, xs_coord, ys_coord, zs_coord, stim_x, stim_y, stim_z, stim_step)
        primal, tangent = jax.jvp(partial(react, stim_count=stim_now), (u_cell, v_gate, w_gate), (du_cell, dv_gate, dw_gate))
        u_cell = primal[0] + spread(c_along, c_across, live, u_pad)
        du_cell = tangent[0] + spread(c_along, c_across, live, du_pad) + spread(d_along, d_across, live, u_pad)
        v_gate, w_gate = (primal[1], primal[2])
        dv_gate, dw_gate = (tangent[1], tangent[2])
        du_saved.append(du_cell)
    mean_weight = jnp.sum(obs_weight) / (NX * NY * NZ)
    scaled = obs_weight / mean_weight
    adj_u = scaled * du_saved[-1]
    adj_v = jnp.zeros(u_start.shape, jnp.float32)
    adj_w = jnp.zeros(u_start.shape, jnp.float32)
    gradient = jnp.zeros(u_start.shape, jnp.float32)
    zero_stim = jnp.zeros(u_start.shape, jnp.float32)
    for step in reversed(range(STEPS)):
        adj_pad = pad_one(adj_u)
        gradient = gradient + sigma_term(along, across, live, u_saved[step], adj_pad)
        if step > 0:
            _, pull = jax.vjp(partial(react, stim_count=zero_stim), shifted(u_saved[step], 0, 0), v_saved[step], w_saved[step])
            back_u, back_v, back_w = pull((adj_u, adj_v, adj_w))
            adj_u = back_u + spread(c_along, c_across, live, adj_pad) + scaled * du_saved[step - 1]
            adj_v, adj_w = (back_v, back_w)
    hess_vec = gradient + tv_weight * tv_apply(sig_pad, dir_pad, live)
    curvature = jnp.sum(direction * hess_vec)
    return (hess_vec, curvature)
```

```python
from functools import partial

import jax
import jax.numpy as jnp
from jax import lax
from jax.sharding import Mesh
from jax.sharding import PartitionSpec as P

STEPS = 4
GX = ("gx_0", "gx_1", "gx_2")


time_step = 0.25
u_crit = 0.13
u_gate = 0.04
switch_width = 0.05
tau_fast = 0.4
tau_open = 12.5
tau_repol = 33.33
tau_slow = 15.0
k_slow = 10.0
u_slow = 0.85
tau_vplus = 3.33
tau_vminus_one = 19.6
tau_vminus_two = 1000.0
tau_wplus = 667.0
tau_wminus = 11.0
stim_amp = 2.0
tv_weight = 0.05
tv_smooth = 0.02


def pair_lists(size):
    even = [(i, i ^ 1) for i in range(size)]
    odd = [(i, (i + 1 if i % 2 else i - 1) % size) for i in range(size)]
    return even, odd


def swap_faces(low, high, axis):
    size = lax.axis_size(axis)
    even, odd = pair_lists(size)
    first = lax.axis_index(axis) % 2 == 0
    to_odd = lax.ppermute(jnp.where(first, low, high), axis, odd)
    to_even = lax.ppermute(jnp.where(first, high, low), axis, even)
    return jnp.where(first, to_odd, to_even), jnp.where(first, to_even, to_odd)


def faces_of(x, axis, dim):
    length = x.shape[dim]
    last = lax.index_in_dim(x, length - 1, axis=dim, keepdims=False)
    leading = lax.index_in_dim(x, 0, axis=dim, keepdims=False)
    low, high = swap_faces(leading, last, axis)
    return jnp.expand_dims(low, dim), jnp.expand_dims(high, dim)


def extended(x, sides, width):
    for axis, dim in sides:
        low, high = faces_of(x, axis, dim)
        x = jnp.concatenate([low, x, high], axis=dim)
    return x


def padded_2(x, sides, width):
    edges = {dim: faces_of(x, axis, dim) for axis, dim in reversed(sides)}
    done = []
    for _, dim in sides:
        low, high = edges[dim]
        around = [(width, width) if d in done else (0, 0) for d in range(x.ndim)]
        x = jnp.concatenate([jnp.pad(low, around), x, jnp.pad(high, around)], axis=dim)
        done.append(dim)
    return x


def butterfly(x, axes):
    for axis in axes:
        size = lax.axis_size(axis)
        step = 1
        while step < size:
            x = x + lax.ppermute(x, axis, [(i, i ^ step) for i in range(size)])
            step *= 2
    return x


def switch(value):
    return 0.5 * (1.0 + jnp.tanh(value / switch_width))


def react(u_cell, v_gate, w_gate, stim_count):
    opened = switch(u_cell - u_crit)
    partly = switch(u_cell - u_gate)
    fast_in = -v_gate * opened * (1.0 - u_cell) * (u_cell - u_crit) / tau_fast
    slow_out = u_cell * (1.0 - opened) / tau_open + opened / tau_repol
    slow_in = -w_gate * (1.0 + jnp.tanh(k_slow * (u_cell - u_slow))) / (2.0 * tau_slow)
    u_next = u_cell + time_step * (stim_amp * stim_count - (fast_in + slow_out + slow_in))
    closed = 1.0 - opened
    v_rate = opened / tau_vplus + closed / (
        partly * tau_vminus_one + (1.0 - partly) * tau_vminus_two
    )
    w_rate = opened / tau_wplus + closed / tau_wminus
    v_next = closed + (v_gate - closed) * jnp.exp(-time_step * v_rate)
    w_next = closed + (w_gate - closed) * jnp.exp(-time_step * w_rate)
    return (u_next, v_next, w_next)


def kappas(tissue):
    scar = (tissue == 0).astype(jnp.float32)
    healthy = (tissue == 1).astype(jnp.float32)
    fiber = (tissue == 2).astype(jnp.float32)
    return (0.1 * scar + healthy + 1.5 * fiber, 0.1 * scar + healthy + 0.75 * fiber)


def shifted(padded, axis, offset):
    index = [
        slice(1, padded.shape[0] - 1),
        slice(1, padded.shape[1] - 1),
        slice(1, padded.shape[2] - 1),
    ]
    index[axis] = slice(1 + offset, padded.shape[axis] - 1 + offset)
    return padded[tuple(index)]


def crop(array, width):
    return array[
        width : array.shape[0] - width,
        width : array.shape[1] - width,
        width : array.shape[2] - width,
    ]


def spread(along_c, across_c, live, values):
    centre = shifted(values, 0, 0)
    result = jnp.zeros(centre.shape, jnp.float32)
    for axis in range(3):
        coeff = along_c if axis == 0 else across_c
        own = shifted(coeff, axis, 0)
        for offset in (1, -1):
            face = 0.5 * (own + shifted(coeff, axis, offset)) * shifted(live, axis, offset)
            result = result + face * (shifted(values, axis, offset) - centre)
    return result


def sigma_term(along, across, live, u_pad, adj_pad):
    u_centre = shifted(u_pad, 0, 0)
    a_centre = shifted(adj_pad, 0, 0)
    parts = []
    for axis in range(3):
        part_sum = jnp.zeros(u_centre.shape, jnp.float32)
        for offset in (1, -1):
            part_sum = part_sum + 0.5 * (shifted(u_pad, axis, offset) - u_centre) * (
                a_centre - shifted(adj_pad, axis, offset)
            ) * shifted(live, axis, offset)
        parts.append(part_sum)
    return along * parts[0] + across * (parts[1] + parts[2])


def forward_diff(padded, live, axis):
    lower = [slice(0, -1), slice(0, -1), slice(0, -1)]
    upper = [slice(0, -1), slice(0, -1), slice(0, -1)]
    upper[axis] = slice(1, None)
    return (padded[tuple(upper)] - padded[tuple(lower)]) * live[tuple(upper)] * live[tuple(lower)]


def tv_apply(sig_pad, dir_pad, live):
    diffs = [forward_diff(sig_pad, live, axis) for axis in range(3)]
    weight = 1.0 / jnp.sqrt(
        diffs[0] * diffs[0] + diffs[1] * diffs[1] + diffs[2] * diffs[2] + tv_smooth * tv_smooth
    )
    result = None
    energy = None
    for axis in range(3):
        flux = weight * forward_diff(dir_pad, live, axis)
        here = flux[1:, 1:, 1:]
        index = [slice(1, None), slice(1, None), slice(1, None)]
        index[axis] = slice(0, -1)
        term = flux[tuple(index)] - here
        result = term if result is None else result + term
        power = here * forward_diff(dir_pad, live, axis)[1:, 1:, 1:]
        energy = power if energy is None else energy + power
    return result, energy


def stimulus(step, xs_coord, ys_coord, zs_coord, stim_x, stim_y, stim_z, stim_step):
    active = (stim_step == step).astype(jnp.float32)
    near_x = (jnp.abs(xs_coord[None, :] - stim_x[:, None]) <= 1).astype(jnp.float32) * active[
        :, None
    ]
    near_y = (jnp.abs(ys_coord[None, :] - stim_y[:, None]) <= 1).astype(jnp.float32)
    near_z = (jnp.abs(zs_coord[None, :] - stim_z[:, None]) <= 1).astype(jnp.float32)
    return jnp.einsum("si,sj,sk->ijk", near_x, near_y, near_z, precision=lax.Precision.HIGHEST)


def advance(u_pad, du_pad, v_gate, w_gate, dv_gate, dw_gate, coeffs, live, stim_now):
    c_along, c_across, d_along, d_across = coeffs
    primal, tangent = jax.jvp(
        partial(react, stim_count=stim_now),
        (crop(u_pad, 1), v_gate, w_gate),
        (crop(du_pad, 1), dv_gate, dw_gate),
    )
    u_next = primal[0] + spread(c_along, c_across, live, u_pad)
    du_next = (
        tangent[0]
        + spread(c_along, c_across, live, du_pad)
        + spread(d_along, d_across, live, u_pad)
    )
    return (u_next, primal[1], primal[2], du_next, tangent[1], tangent[2])


def shards(
    u_start,
    v_start,
    w_start,
    conduct,
    direction,
    obs_weight,
    tissue,
    stim_x,
    stim_y,
    stim_z,
    stim_step,
):
    shapes = u_start.shape
    anchor = (
        lax.axis_index(GX) * shapes[0],
        lax.axis_index("gy") * shapes[1],
        lax.axis_index("gz") * shapes[2],
    )
    limits = (
        shapes[0] * lax.axis_size(GX),
        shapes[1] * lax.axis_size("gy"),
        shapes[2] * lax.axis_size("gz"),
    )
    voxels = limits[0] * limits[1] * limits[2]
    along, across = kappas(tissue)

    def grid_at(width):
        vectors = []
        flags = []
        for axis in range(3):
            coord = anchor[axis] - width + jnp.arange(shapes[axis] + 2 * width, dtype=jnp.int32)
            vectors.append(coord)
            flags.append(((coord >= 0) & (coord < limits[axis])).astype(jnp.float32))
        live = flags[0][:, None, None] * flags[1][None, :, None] * flags[2][None, None, :]
        return (vectors, live)

    inner_vectors, unused_live = grid_at(0)
    outer_vectors, live_one = grid_at(1)
    u_saved, v_saved, w_saved, du_saved = ([], [], [], [])
    static = extended(
        jnp.stack([conduct, direction, along, across, u_start]), ((GX, 1), ("gy", 2), ("gz", 3)), 1
    )
    sig_pad, dir_pad, along_pad, across_pad, u_pad = (
        static[0],
        static[1],
        static[2],
        static[3],
        static[4],
    )
    coeffs = (along_pad * sig_pad, across_pad * sig_pad, along_pad * dir_pad, across_pad * dir_pad)
    du_pad = jnp.zeros(u_pad.shape, jnp.float32)
    v_gate, w_gate = (v_start, w_start)
    dv_gate = jnp.zeros(shapes, jnp.float32)
    dw_gate = jnp.zeros(shapes, jnp.float32)
    for step in range(STEPS):
        u_saved.append(u_pad)
        v_saved.append(v_gate)
        w_saved.append(w_gate)
        u_cell, v_gate, w_gate, du_cell, dv_gate, dw_gate = advance(
            u_pad,
            du_pad,
            v_gate,
            w_gate,
            dv_gate,
            dw_gate,
            coeffs,
            live_one,
            stimulus(
                step,
                inner_vectors[0],
                inner_vectors[1],
                inner_vectors[2],
                stim_x,
                stim_y,
                stim_z,
                stim_step,
            ),
        )
        du_saved.append(du_cell)
        if step + 1 < STEPS:
            moved = padded_2(jnp.stack([u_cell, du_cell]), ((GX, 1), ("gy", 2), ("gz", 3)), 1)
            u_pad, du_pad = (moved[0], moved[1])
    prior, energy = tv_apply(sig_pad, dir_pad, live_one)
    squares = sum(du * du for du in du_saved)
    sums = jnp.stack([jnp.sum(obs_weight), jnp.sum(obs_weight * squares), jnp.sum(energy)])
    sums = butterfly(sums, ("gx_2", "gz", "gy", "gx_0", "gx_1"))
    c_along, c_across = (coeffs[0], coeffs[1])
    adj_u = obs_weight * du_saved[-1]
    adj_v = jnp.zeros(shapes, jnp.float32)
    adj_w = jnp.zeros(shapes, jnp.float32)
    gradient = jnp.zeros(shapes, jnp.float32)
    zero_stim = jnp.zeros(shapes, jnp.float32)
    for step in reversed(range(STEPS)):
        adj_pad = padded_2(adj_u, ((GX, 0), ("gy", 1), ("gz", 2)), 1)
        gradient = gradient + sigma_term(along, across, live_one, u_saved[step], adj_pad)
        if step > 0:
            _, pull = jax.vjp(
                partial(react, stim_count=zero_stim),
                crop(u_saved[step], 1),
                v_saved[step],
                w_saved[step],
            )
            back_u, back_v, back_w = pull((adj_u, adj_v, adj_w))
            adj_u = (
                back_u
                + spread(c_along, c_across, live_one, adj_pad)
                + obs_weight * du_saved[step - 1]
            )
            adj_v, adj_w = (back_v, back_w)
    factor = voxels / sums[0]
    hess_vec = gradient * factor + tv_weight * prior
    curvature = sums[1] * factor + tv_weight * sums[2]
    return (hess_vec, curvature)


def solution(mesh):
    split = Mesh(
        mesh.devices.reshape(4, 2, 2, mesh.shape["gy"], mesh.shape["gz"]),
        ("gx_0", "gx_1", "gx_2", "gy", "gz"),
    )
    in_specs = (
        P(GX, "gy", "gz"),
        P(GX, "gy", "gz"),
        P(GX, "gy", "gz"),
        P(GX, "gy", "gz"),
        P(GX, "gy", "gz"),
        P(GX, "gy", "gz"),
        P(GX, "gy", "gz"),
        P(),
        P(),
        P(),
        P(),
    )
    out_specs = (P(GX, "gy", "gz"), P())
    return jax.shard_map(
        shards, mesh=split, in_specs=in_specs, out_specs=out_specs, check_vma=False
    )
```
